128 devices in a mesh: grp: 2 (over y_lo), sp: 64 (over x, y_hi, z, core).
Axes of the slice: x: 4, y: 4 (y_hi: 2, y_lo: 2; y = y_hi * 2 + y_lo), z: 4, core: 2. Of those that a mesh axis runs over, the one named last changes fastest.
Arguments:
- modes: bfloat16 [3, 512, 32, 16, 256], P(None, 'sp', 'grp'), may hold values from -16 to 16
- convecting: int32 [12], replicated, may hold values from 0 to 255, as said below
Outputs:
- skew_tensor: float32 [12, 256, 256], P(None, 'sp')
The draws below stay inside these ranges and needn't reach their ends.
Inputs may be any that keep to these rules, and one draw needn't show every extreme that they name: `convecting`: 12 distinct mode indices.
All inputs are finite; a program needn't handle non-finite values.
Results may differ from the reference program's by a relative error of at most 0.0029.
Values may be sent and summed in bfloat16 or wider, within the bound.
No kernel may reach another device: no remote copies, remote signals or barrier semaphores. Data moves between devices by JAX's collectives and lax.ppermute only.
A program may use at most 64 MiB of HBM per device.

```python
import math
import jax
import jax.numpy as jnp
from jax import lax

M = 256
NSEL = 12
CX = 8
NZ = 16
NX = 512
NY = 32


def draw_convecting(key, part):
    return jax.random.permutation(jax.random.fold_in(key, 7), M)[:NSEL].astype(jnp.int32)


def raised(entries, own_key, source, target, parts, factor):
    def block_of(position):
        return (jnp.arange(entries.shape[position]) // (entries.shape[position] // parts)).reshape((-1,) + (1,) * (entries.ndim - 1 - position))

    near = jax.random.permutation(own_key, parts)[block_of(target)]
    other_side = (block_of(target) + parts // 2) % parts
    return jnp.where((block_of(source) == near) | (block_of(source) == other_side), factor * entries, entries)


def steps_of(rng, shape, cuts, low, top_value):
    level = 1.0
    for axis_at, parts in cuts:
        heights = jax.random.uniform(jax.random.fold_in(jax.random.fold_in(rng, 6), axis_at), (parts,), jnp.float32, low / len(cuts), top_value / len(cuts))
        level = level * jnp.repeat(jnp.exp(heights), shape[axis_at] // parts).reshape((-1,) + (1,) * (len(shape) - 1 - axis_at))
    return level


def heavy_noise(key, dims, deviation, bound, split, heavy, held_as=jnp.bfloat16):
    values = deviation * jax.random.normal(key, dims, jnp.float32)
    if split:
        values = values * steps_of(key, dims, split, -0.22, 0.18)
    return jnp.clip(raised(values, jax.random.fold_in(key, 3), *heavy), -bound, bound).astype(held_as)


def setup_inputs(seed: int = 0) -> dict:
    keys = jax.random.split(jax.random.key(seed), 3)
    modes = heavy_noise(keys[0], (3, NX, NY, NZ, M), 1.0, 16.0, ((1, 64), (2, 2)), (1, 4, 64, 4.0))
    convecting = draw_convecting(jax.random.fold_in(keys[2], 71), 0)
    return dict(modes=modes, convecting=convecting)


def reference(modes, convecting):
    cells = NX * NY * NZ
    padded = jnp.concatenate([modes[:, -1:], modes, modes[:, :1]], axis=1)
    slabs = NX // CX

    def one_slab(total, index):
        window = lax.dynamic_slice_in_dim(padded, (index * CX).astype(jnp.int32), CX + 2, 1)
        widened = window.astype(jnp.float32)
        centre = widened[:, 1:-1]
        along_x = widened[:, 2:] - widened[:, :-2]
        along_y = jnp.roll(centre, -1, axis=2) - jnp.roll(centre, 1, axis=2)
        along_z = jnp.roll(centre, -1, axis=3) - jnp.roll(centre, 1, axis=3)
        velocity = jnp.take(centre, convecting, axis=4)
        test_flat = centre.reshape(-1, M)

        def per_mode(select):
            field = lax.dynamic_index_in_dim(velocity, select, 4, keepdims=False)
            moved = 0.5 * (field[0][..., None] * along_x + field[1][..., None] * along_y + field[2][..., None] * along_z)
            moved = moved.astype(jnp.bfloat16).astype(jnp.float32).reshape(-1, M)
            return jnp.dot(test_flat.T, moved, precision=lax.Precision.HIGHEST, preferred_element_type=jnp.float32)
        part = lax.map(per_mode, jnp.arange(NSEL, dtype=jnp.int32))
        return (total + part, None)
    total, _ = lax.scan(one_slab, jnp.zeros((NSEL, M, M), jnp.float32), jnp.arange(slabs, dtype=jnp.int32))
    tensor = total / math.sqrt(cells)
    return 0.5 * (tensor - jnp.swapaxes(tensor, 1, 2))
```

```python
import jax
import jax.numpy as jnp
from jax import lax
from jax.experimental import pallas as pl
from jax.experimental.pallas import tpu as pltpu
from jax.sharding import Mesh, PartitionSpec as P

M = 256
NSEL = 12
HALF = NSEL // 2
CX, CY, NZ = 8, 16, 16
BLOCK = CY * NZ
SP = ("x", "yh", "z", "core")
VMEM_LIMIT = 44 * 1024 * 1024


def constants(conv, picker, shift):
    lane = lax.broadcasted_iota(jnp.int32, (1, 128), 1)
    wanted = jnp.full((1, 128), -1, jnp.int32)
    for a in range(NSEL):
        wanted = jnp.where(lane == a, conv[a], wanted)
    row = lax.broadcasted_iota(jnp.int32, (M, 128), 0)
    picker[...] = jnp.where(row == wanted, 1.0, 0.0).astype(jnp.bfloat16)
    row = lax.broadcasted_iota(jnp.int32, (BLOCK, BLOCK), 0)
    col = lax.broadcasted_iota(jnp.int32, (BLOCK, BLOCK), 1)
    base = row - row % NZ
    after = col == base + (row + 1) % NZ
    before = col == base + (row + NZ - 1) % NZ
    shift[...] = jnp.where(after, 1.0, jnp.where(before, -1.0, 0.0)).astype(jnp.bfloat16)


def prepare(rows, picker, shift, vel, dzs, mt):
    n = rows[0].shape[0]
    for c in range(3):
        vel[c, 0:n] = jnp.dot(rows[c], picker[...], preferred_element_type=jnp.float32)
        dzs[c, 0:n] = jnp.dot(shift[0:n, 0:n], rows[c], preferred_element_type=jnp.float32)
        mt[:, c * n : (c + 1) * n] = rows[c].T


def advect(ext, x, y, t, n, vel, dzs, mv):
    here = slice(t * NZ, (t + 1) * NZ)
    speeds = [vel[d, here] for d in range(3)]
    for h in range(2):
        lanes = slice(h * 128, (h + 1) * 128)
        fields = []
        for c in range(3):
            dx = ext[c, x + 1, y, :, lanes].astype(jnp.float32) - ext[c, x - 1, y, :, lanes].astype(jnp.float32)
            dy = ext[c, x, y + 1, :, lanes].astype(jnp.float32) - ext[c, x, y - 1, :, lanes].astype(jnp.float32)
            fields.append((dx, dy, dzs[c, here, lanes]))
        for a in range(NSEL):
            u, v, w = (jnp.broadcast_to(s[:, a : a + 1], (NZ, 128)) for s in speeds)
            for c, (dx, dy, dz) in enumerate(fields):
                moved = u * dx + v * dy + w * dz
                mv[a, c * n + t * NZ : c * n + (t + 1) * NZ, lanes] = moved.astype(jnp.bfloat16)


def product(a, n, mt, mv, source, acc):
    acc[a] = source[a] + jnp.dot(mt[:, 0 : 3 * n], mv[a, 0 : 3 * n], preferred_element_type=jnp.float32)


def interleave(tiles, dots):
    done = 0
    for k, tile in enumerate(tiles):
        tile()
        upto = (k + 1) * len(dots) // len(tiles)
        for dot in dots[done:upto]:
            dot()
        done = upto
    for dot in dots[done:]:
        dot()


def interior_kernel(conv, modes, acc, ext, picker, shift, vel, dzs, mt_a, mt_b, mv_a, mv_b, sems):
    copies = [pltpu.make_async_copy(modes.at[:, x], ext.at[:, x], sems.at[x]) for x in range(CX)]
    for copy in copies:
        copy.start()
    constants(conv, picker, shift)
    acc[...] = jnp.zeros_like(acc)
    blank = jnp.zeros((NSEL, NZ, M), jnp.bfloat16)
    for mv in (mv_a, mv_b):
        for c in range(3):
            mv[:, c * BLOCK : c * BLOCK + NZ] = blank
            mv[:, (c + 1) * BLOCK - NZ : (c + 1) * BLOCK] = blank
    for copy in copies:
        copy.wait()

    def stage(x, mt_w, mv_w, mt_r, mv_r):
        dots = []
        if mv_r is not None:
            dots = [lambda a=a: product(a, BLOCK, mt_r, mv_r, acc, acc) for a in range(NSEL)]
        tiles = []
        if mv_w is not None:
            rows = [ext[c, x].reshape(BLOCK, M) for c in range(3)]
            prepare(rows, picker, shift, vel, dzs, mt_w)
            tiles = [lambda y=y: advect(ext, x, y, y, BLOCK, vel, dzs, mv_w) for y in range(1, CY - 1)]
        interleave(tiles, dots)

    stage(1, mt_a, mv_a, None, None)

    def pair(j, carry):
        stage(2 * j + 2, mt_b, mv_b, mt_a, mv_a)
        stage(2 * j + 3, mt_a, mv_a, mt_b, mv_b)
        return carry

    lax.fori_loop(0, 2, pair, 0)
    stage(6, mt_b, mv_b, mt_a, mv_a)
    stage(None, None, None, mt_b, mv_b)


def boundary_kernel(conv, core, modes, near, far, yface, start, theirs, mine,
                    ext, picker, shift, vel, dzs, acc, mt_a, mt_b, mv_a, mv_b, sems):
    me = core[0]
    copies = [pltpu.make_async_copy(modes.at[:, x], ext.at[:, x + 1, 1:17], sems.at[x]) for x in range(CX)]
    copies += [
        pltpu.make_async_copy(near, ext.at[:, pl.ds(9 - 9 * me, 1), 1:17], sems.at[8]),
        pltpu.make_async_copy(far, ext.at[:, pl.ds(9 * me, 1), 1:17], sems.at[9]),
        pltpu.make_async_copy(yface.at[:, :, 0:1], ext.at[:, 1:9, 0:1], sems.at[10]),
        pltpu.make_async_copy(yface.at[:, :, 1:2], ext.at[:, 1:9, 17:18], sems.at[11]),
    ]
    for copy in copies:
        copy.start()
    constants(conv, picker, shift)
    for copy in copies:
        copy.wait()

    edge = [(x, y) for y in (1, CY) for x in range(2, CX)]
    plane = [[(x, y) for y in range(1, CY + 1)] for x in (1, CX)]
    work = [edge] + plane
    buffers = [(mt_a, mv_a), (mt_b, mv_b), (mt_a, mv_a)]
    for k in range(4):
        dots, tiles = [], []
        if k > 0:
            n_r = len(work[k - 1]) * NZ
            mt_r, mv_r = buffers[k - 1]
            source = start if k == 1 else acc
            dots = [
                lambda a=a, n_r=n_r, mt_r=mt_r, mv_r=mv_r, source=source: product(a, n_r, mt_r, mv_r, source, acc)
                for a in range(NSEL)
            ]
        if k < 3:
            n = len(work[k]) * NZ
            mt_w, mv_w = buffers[k]
            if k == 0:
                rows = [
                    jnp.concatenate([ext[c, 2:CX, y].reshape(n // 2, M) for y in (1, CY)], axis=0) for c in range(3)
                ]
            else:
                rows = [ext[c, work[k][0][0], 1 : CY + 1].reshape(n, M) for c in range(3)]
            prepare(rows, picker, shift, vel, dzs, mt_w)
            tiles = [
                lambda x=x, y=y, t=t, n=n, mv_w=mv_w: advect(ext, x, y, t, n, vel, dzs, mv_w)
                for t, (x, y) in enumerate(work[k])
            ]
        interleave(tiles, dots)

    def finish(j, carry):
        block = acc[(1 - me) * HALF + j]
        theirs[j] = (block - block.T).astype(jnp.bfloat16)
        return carry

    def keep(j, carry):
        block = acc[me * HALF + j]
        mine[j] = block - block.T
        return carry

    lax.fori_loop(0, HALF, finish, 0)
    lax.fori_loop(0, HALF, keep, 0)


SMEM = pl.BlockSpec(memory_space=pltpu.SMEM)
HBM = pl.BlockSpec(memory_space=pl.ANY)
VMEM = pl.BlockSpec(memory_space=pltpu.VMEM)
WORK = [
    pltpu.VMEM((M, 128), jnp.bfloat16),
    pltpu.VMEM((BLOCK, BLOCK), jnp.bfloat16),
    pltpu.VMEM((3, BLOCK, 128), jnp.float32),
    pltpu.VMEM((3, BLOCK, M), jnp.float32),
]
BUFFERS = [pltpu.VMEM((M, 3 * BLOCK), jnp.bfloat16)] * 2 + [pltpu.VMEM((NSEL, 3 * BLOCK, M), jnp.bfloat16)] * 2


def interior(convecting, modes):
    return pl.pallas_call(
        interior_kernel,
        out_shape=pltpu.VMEM((NSEL, M, M), jnp.float32),
        in_specs=[SMEM, HBM],
        out_specs=VMEM,
        scratch_shapes=[pltpu.VMEM((3, CX, CY, NZ, M), jnp.bfloat16)] + WORK + BUFFERS + [pltpu.SemaphoreType.DMA((CX,))],
        compiler_params=pltpu.CompilerParams(vmem_limit_bytes=VMEM_LIMIT),
        name="interior",
    )(convecting, modes)


def boundary(convecting, core, modes, near, far, yface, start):
    return pl.pallas_call(
        boundary_kernel,
        out_shape=(
            jax.ShapeDtypeStruct((HALF, M, M), jnp.bfloat16),
            jax.ShapeDtypeStruct((HALF, M, M), jnp.float32),
        ),
        in_specs=[SMEM, SMEM, HBM, HBM, HBM, HBM, VMEM],
        out_specs=(VMEM, VMEM),
        scratch_shapes=[pltpu.VMEM((3, CX + 2, CY + 2, NZ, M), jnp.bfloat16)] + WORK
        + [pltpu.VMEM((NSEL, M, M), jnp.float32)] + BUFFERS + [pltpu.SemaphoreType.DMA((12,))],
        compiler_params=pltpu.CompilerParams(vmem_limit_bytes=VMEM_LIMIT),
        name="boundary",
    )(convecting, core, modes, near, far, yface, start)


def shards(modes, convecting):
    swap = [(0, 1), (1, 0)]
    across = [(s, (s + 1) % 64 if s % 2 else (s - 1) % 64) for s in range(64)]
    core = lax.axis_index("core")
    last = (CX - 1) * core
    far = lax.ppermute(lax.dynamic_slice_in_dim(modes, last, 1, 1), SP, across)
    near = lax.ppermute(lax.dynamic_slice_in_dim(modes, CX - 1 - last, 1, 1), "core", swap)
    yface = lax.ppermute(jnp.concatenate([modes[:, :, -1:], modes[:, :, :1]], axis=2), "yl", swap)
    start = interior(convecting, modes)
    theirs, mine = boundary(convecting, core.reshape(1).astype(jnp.int32), modes, near, far, yface, start)
    paired = (mine + lax.ppermute(theirs, "core", swap).astype(jnp.float32)).astype(jnp.bfloat16)
    spread = lax.all_to_all(paired, SP, split_axis=1, concat_axis=0, tiled=True)
    owned = spread.reshape(32, NSEL, 4, M).astype(jnp.float32).sum(0)
    owned = owned + lax.ppermute(owned, "yl", swap)
    return owned * (0.25 / 512.0)


def solution(mesh):
    fine = Mesh(mesh.devices.reshape(2, 4, 2, 4, 2), ("yl",) + SP)
    placed = (P(None, SP, "yl", None, None), P())
    return jax.shard_map(
        shards, mesh=fine, in_specs=placed, out_specs=P(None, SP, None), check_vma=False
    )
```

```python
import jax
import jax.numpy as jnp
from jax import lax
from jax.experimental import pallas as pl
from jax.experimental.pallas import tpu as pltpu
from jax.sharding import Mesh, PartitionSpec as P

M = 256
NSEL = 12
HALF = NSEL // 2
GROUP = 4
CX, CY, NZ = 8, 16, 16
BLOCK = CY * NZ
SP = ("x", "yh", "z", "core")
VMEM_LIMIT = 44 * 1024 * 1024


def constants(conv, picker, shift):
    lane = lax.broadcasted_iota(jnp.int32, (1, 128), 1)
    wanted = jnp.full((1, 128), -1, jnp.int32)
    for a in range(NSEL):
        wanted = jnp.where(lane == a, conv[a], wanted)
    row = lax.broadcasted_iota(jnp.int32, (M, 128), 0)
    picker[...] = jnp.where(row == wanted, 1.0, 0.0).astype(jnp.bfloat16)
    row = lax.broadcasted_iota(jnp.int32, (BLOCK, BLOCK), 0)
    col = lax.broadcasted_iota(jnp.int32, (BLOCK, BLOCK), 1)
    base = row - row % NZ
    after = col == base + (row + 1) % NZ
    before = col == base + (row + NZ - 1) % NZ
    shift[...] = jnp.where(after, 1.0, jnp.where(before, -1.0, 0.0)).astype(jnp.bfloat16)


def prepare(rows, picker, shift, vel, fld, mt):
    n = rows[0].shape[0]
    for c in range(3):
        vel[c, 0:n] = jnp.dot(rows[c], picker[...], preferred_element_type=jnp.float32)
        fld[2, c, 0:n] = jnp.dot(shift[0:n, 0:n], rows[c], preferred_element_type=jnp.float32)
        mt[:, c * n : (c + 1) * n] = rows[c].T


def difference(at, x, y, t, fld):
    here = slice(t * NZ, (t + 1) * NZ)
    for c in range(3):
        fld[0, c, here] = at(c, x + 1, y).astype(jnp.float32) - at(c, x - 1, y).astype(jnp.float32)
        fld[1, c, here] = at(c, x, y + 1).astype(jnp.float32) - at(c, x, y - 1).astype(jnp.float32)


def advect(t, n, vel, fld, mv, group):
    here = slice(t * NZ, (t + 1) * NZ)
    chosen = range(group * GROUP, (group + 1) * GROUP)
    speeds = [vel[d, here] for d in range(3)]
    wide = [[jnp.broadcast_to(s[:, a : a + 1], (NZ, 128)) for s in speeds] for a in chosen]
    for c in range(3):
        for h in range(2):
            lanes = slice(h * 128, (h + 1) * 128)
            dx, dy, dz = (fld[d, c, here, lanes] for d in range(3))
            for a, (u, v, w) in zip(chosen, wide):
                moved = u * dx + v * dy + w * dz
                mv[a, c * n + t * NZ : c * n + (t + 1) * NZ, lanes] = moved.astype(jnp.bfloat16)


def product(a, n, mt, mv, source, acc):
    acc[a] = source[a] + jnp.dot(mt[:, 0 : 3 * n], mv[a, 0 : 3 * n], preferred_element_type=jnp.float32)


def interleave(items, dots):
    done = 0
    for k, item in enumerate(items):
        item()
        upto = (k + 1) * len(dots) // len(items)
        for dot in dots[done:upto]:
            dot()
        done = upto
    for dot in dots[done:]:
        dot()


def works(at, tiles, n, vel, fld, mv):
    items = []
    for t, (x, y) in tiles:
        items.append(lambda x=x, y=y, t=t: difference(at, x, y, t, fld))
    for t, _ in tiles:
        for group in range(NSEL // GROUP):
            items.append(lambda t=t, group=group: advect(t, n, vel, fld, mv, group))
    return items


def interior_kernel(conv, modes, acc, picker, shift, vel, fld, mt_a, mt_b, mv_a, mv_b):
    constants(conv, picker, shift)
    acc[...] = jnp.zeros_like(acc)
    blank = jnp.zeros((NSEL, NZ, M), jnp.bfloat16)
    for mv in (mv_a, mv_b):
        for c in range(3):
            mv[:, c * BLOCK : c * BLOCK + NZ] = blank
            mv[:, (c + 1) * BLOCK - NZ : (c + 1) * BLOCK] = blank

    def at(c, x, y):
        return modes[c, x, y]

    def stage(x, mt_w, mv_w, mt_r, mv_r):
        dots = []
        if mv_r is not None:
            dots = [lambda a=a: product(a, BLOCK, mt_r, mv_r, acc, acc) for a in range(NSEL)]
        items = []
        if mv_w is not None:
            prepare([modes[c, x].reshape(BLOCK, M) for c in range(3)], picker, shift, vel, fld, mt_w)
            items = works(at, [(y, (x, y)) for y in range(1, CY - 1)], BLOCK, vel, fld, mv_w)
        interleave(items, dots)

    stage(1, mt_a, mv_a, None, None)

    def pair(j, carry):
        stage(2 * j + 2, mt_b, mv_b, mt_a, mv_a)
        stage(2 * j + 3, mt_a, mv_a, mt_b, mv_b)
        return carry

    lax.fori_loop(0, 2, pair, 0)
    stage(6, mt_b, mv_b, mt_a, mv_a)
    stage(None, None, None, mt_b, mv_b)


def boundary_kernel(conv, core, modes, near, far, yface, start, theirs, mine,
                    xface, picker, shift, vel, fld, acc, mt_a, mt_b, mv_a, mv_b):
    me = core[0]
    constants(conv, picker, shift)
    xface[:, pl.ds(1 - me, 1)] = near[...]
    xface[:, pl.ds(me, 1)] = far[...]

    def at(c, x, y):
        if x in (-1, CX):
            return xface[c, 1 if x == CX else 0, y]
        if y in (-1, CY):
            return yface[c, x, 1 if y == CY else 0]
        return modes[c, x, y]

    edge = [(x, y) for y in (0, CY - 1) for x in range(1, CX - 1)]
    plane = [[(x, y) for y in range(CY)] for x in (0, CX - 1)]
    work = [edge] + plane
    buffers = [(mt_a, mv_a), (mt_b, mv_b), (mt_a, mv_a)]
    for k in range(4):
        dots, items = [], []
        if k > 0:
            n_r = len(work[k - 1]) * NZ
            mt_r, mv_r = buffers[k - 1]
            source = start if k == 1 else acc
            dots = [
                lambda a=a, n_r=n_r, mt_r=mt_r, mv_r=mv_r, source=source: product(a, n_r, mt_r, mv_r, source, acc)
                for a in range(NSEL)
            ]
        if k < 3:
            n = len(work[k]) * NZ
            mt_w, mv_w = buffers[k]
            if k == 0:
                rows = [
                    jnp.concatenate([modes[c, 1 : CX - 1, y].reshape(n // 2, M) for y in (0, CY - 1)], axis=0)
                    for c in range(3)
                ]
            else:
                rows = [modes[c, work[k][0][0]].reshape(n, M) for c in range(3)]
            prepare(rows, picker, shift, vel, fld, mt_w)
            items = works(at, list(enumerate(work[k])), n, vel, fld, mv_w)
        interleave(items, dots)

    def finish(j, carry):
        block = acc[(1 - me) * HALF + j]
        theirs[j] = (block - block.T).astype(jnp.bfloat16)
        return carry

    def keep(j, carry):
        block = acc[me * HALF + j]
        mine[j] = block - block.T
        return carry

    lax.fori_loop(0, HALF, finish, 0)
    lax.fori_loop(0, HALF, keep, 0)


def faces_kernel(core, modes, near, far, yface, sems):
    last = (CX - 1) * core[0]
    copies = [
        pltpu.make_async_copy(modes.at[:, pl.ds(last, 1)], far, sems.at[0]),
        pltpu.make_async_copy(modes.at[:, pl.ds(CX - 1 - last, 1)], near, sems.at[1]),
        pltpu.make_async_copy(modes.at[:, :, CY - 1 : CY], yface.at[:, :, 0:1], sems.at[2]),
        pltpu.make_async_copy(modes.at[:, :, 0:1], yface.at[:, :, 1:2], sems.at[3]),
    ]
    for copy in copies:
        copy.start()
    for copy in copies:
        copy.wait()


SMEM = pl.BlockSpec(memory_space=pltpu.SMEM)
HBM = pl.BlockSpec(memory_space=pl.ANY)
VMEM = pl.BlockSpec(memory_space=pltpu.VMEM)
WORK = [
    pltpu.VMEM((M, 128), jnp.bfloat16),
    pltpu.VMEM((BLOCK, BLOCK), jnp.bfloat16),
    pltpu.VMEM((3, BLOCK, 128), jnp.float32),
    pltpu.VMEM((3, 3, BLOCK, M), jnp.float32),
]
BUFFERS = [pltpu.VMEM((M, 3 * BLOCK), jnp.bfloat16)] * 2 + [pltpu.VMEM((NSEL, 3 * BLOCK, M), jnp.bfloat16)] * 2


def faces(core, modes):
    return pl.pallas_call(
        faces_kernel,
        out_shape=(
            pltpu.VMEM((3, 1, CY, NZ, M), jnp.bfloat16),
            pltpu.VMEM((3, 1, CY, NZ, M), jnp.bfloat16),
            pltpu.VMEM((3, CX, 2, NZ, M), jnp.bfloat16),
        ),
        in_specs=[SMEM, HBM],
        out_specs=(VMEM, VMEM, VMEM),
        scratch_shapes=[pltpu.SemaphoreType.DMA((4,))],
        compiler_params=pltpu.CompilerParams(vmem_limit_bytes=VMEM_LIMIT),
        name="faces",
    )(core, modes)


def interior(convecting, modes):
    return pl.pallas_call(
        interior_kernel,
        out_shape=pltpu.VMEM((NSEL, M, M), jnp.float32),
        in_specs=[SMEM, VMEM],
        out_specs=VMEM,
        scratch_shapes=WORK + BUFFERS,
        compiler_params=pltpu.CompilerParams(vmem_limit_bytes=VMEM_LIMIT),
        name="interior",
    )(convecting, modes)


def boundary(convecting, core, modes, near, far, yface, start):
    return pl.pallas_call(
        boundary_kernel,
        out_shape=(pltpu.VMEM((HALF, M, M), jnp.bfloat16), pltpu.VMEM((HALF, M, M), jnp.float32)),
        in_specs=[SMEM, SMEM] + [VMEM] * 5,
        out_specs=(VMEM, VMEM),
        scratch_shapes=[pltpu.VMEM((3, 2, CY, NZ, M), jnp.bfloat16)] + WORK
        + [pltpu.VMEM((NSEL, M, M), jnp.float32)] + BUFFERS,
        compiler_params=pltpu.CompilerParams(vmem_limit_bytes=VMEM_LIMIT),
        name="boundary",
    )(convecting, core, modes, near, far, yface, start)


def shards(modes, convecting):
    swap = [(0, 1), (1, 0)]
    across = [(s, (s + 1) % 64 if s % 2 else (s - 1) % 64) for s in range(64)]
    core = lax.axis_index("core").reshape(1).astype(jnp.int32)
    near, far, yface = faces(core, modes)
    far = lax.ppermute(far, SP, across)
    near = lax.ppermute(near, "core", swap)
    yface = lax.ppermute(yface, "yl", swap)
    start = interior(convecting, modes)
    theirs, mine = boundary(convecting, core, modes, near, far, yface, start)
    paired = (mine + lax.ppermute(theirs, "core", swap).astype(jnp.float32)).astype(jnp.bfloat16)
    spread = lax.all_to_all(paired, SP, split_axis=1, concat_axis=0, tiled=True)
    owned = spread.reshape(32, NSEL, 4, M).astype(jnp.float32).sum(0)
    owned = owned + lax.ppermute(owned, "yl", swap)
    return owned * (0.25 / 512.0)


def solution(mesh):
    fine = Mesh(mesh.devices.reshape(2, 4, 2, 4, 2), ("yl",) + SP)
    placed = (P(None, SP, "yl", None, None), P())
    return jax.shard_map(
        shards, mesh=fine, in_specs=placed, out_specs=P(None, SP, None), check_vma=False
    )
```

```python
import jax
import jax.numpy as jnp
from jax import lax
from jax.experimental import pallas as pl
from jax.experimental.pallas import tpu as pltpu
from jax.sharding import Mesh, PartitionSpec as P

M = 256
NSEL = 12
CX, CY, NZ = 8, 16, 16
BLOCK = CY * NZ
SP = ("x", "yh", "z", "core")
VMEM_LIMIT = 44 * 1024 * 1024


def constants(conv, picker, shift):
    lane = lax.broadcasted_iota(jnp.int32, (1, 128), 1)
    wanted = jnp.full((1, 128), -1, jnp.int32)
    for a in range(NSEL):
        wanted = jnp.where(lane == a, conv[a], wanted)
    row = lax.broadcasted_iota(jnp.int32, (M, 128), 0)
    picker[...] = jnp.where(row == wanted, 1.0, 0.0).astype(jnp.bfloat16)
    row = lax.broadcasted_iota(jnp.int32, (BLOCK, BLOCK), 0)
    col = lax.broadcasted_iota(jnp.int32, (BLOCK, BLOCK), 1)
    base = row - row % NZ
    after = col == base + (row + 1) % NZ
    before = col == base + (row + NZ - 1) % NZ
    shift[...] = jnp.where(after, 1.0, jnp.where(before, -1.0, 0.0)).astype(jnp.bfloat16)


def survey(rows, picker, shift, vel, dz):
    n = rows[0].shape[0]
    for c in range(3):
        vel[c, 0:n] = jnp.dot(rows[c], picker[...], preferred_element_type=jnp.float32)
        dz[c, 0:n] = jnp.dot(shift[0:n, 0:n], rows[c], preferred_element_type=jnp.float32)


def transpose(rows, mt):
    n = rows[0].shape[0]
    for c in range(3):
        mt[:, c * n : (c + 1) * n] = rows[c].T


def advect(at, x, y, t, n, vel, dzs, mv):
    here = slice(t * NZ, (t + 1) * NZ)
    speeds = [vel[d, here] for d in range(3)]
    for h in range(2):
        lanes = slice(h * 128, (h + 1) * 128)
        fields = []
        for c in range(3):
            dx = at(c, x + 1, y, lanes).astype(jnp.float32) - at(c, x - 1, y, lanes).astype(jnp.float32)
            dy = at(c, x, y + 1, lanes).astype(jnp.float32) - at(c, x, y - 1, lanes).astype(jnp.float32)
            fields.append((dx, dy, dzs[c, here, lanes]))
        for a in range(NSEL):
            u, v, w = (jnp.broadcast_to(s[:, a : a + 1], (NZ, 128)) for s in speeds)
            for c, (dx, dy, dz) in enumerate(fields):
                moved = u * dx + v * dy + w * dz
                mv[a, c * n + t * NZ : c * n + (t + 1) * NZ, lanes] = moved.astype(jnp.bfloat16)


def product(a, n, mt, mv, source, acc):
    block = jnp.dot(mt[:, 0 : 3 * n], mv[a, 0 : 3 * n], preferred_element_type=jnp.float32)
    acc[a] = block if source is None else source[a] + block


def interleave(items, dots):
    done = 0
    for k, item in enumerate(items):
        item()
        upto = (k + 1) * len(dots) // len(items)
        for dot in dots[done:upto]:
            dot()
        done = upto
    for dot in dots[done:]:
        dot()


def works(at, tiles, n, vel, dz, mv):
    return [lambda x=x, y=y, t=t: advect(at, x, y, t, n, vel, dz, mv) for t, (x, y) in tiles]


def interior_kernel(conv, modes, acc, picker, shift, vel_a, vel_b, dz_a, dz_b, mt_a, mt_b, mv_a, mv_b):
    constants(conv, picker, shift)
    blank = jnp.zeros((NSEL, NZ, M), jnp.bfloat16)
    for mv in (mv_a, mv_b):
        for c in range(3):
            mv[:, c * BLOCK : c * BLOCK + NZ] = blank
            mv[:, (c + 1) * BLOCK - NZ : (c + 1) * BLOCK] = blank
    sets = [(vel_a, dz_a, mt_a, mv_a), (vel_b, dz_b, mt_b, mv_b)]

    def at(c, x, y, lanes):
        return modes[c, x, y, :, lanes]

    def plane(x):
        return [modes[c, x].reshape(BLOCK, M) for c in range(3)]

    def stage(x, side, dots=True, first=False, last=False):
        vel, dz, mt, mv = sets[side]
        vel_n, dz_n, mt_r, mv_r = sets[1 - side]
        todo = []
        if dots:
            source = None if first else acc
            todo = [lambda a=a: product(a, BLOCK, mt_r, mv_r, source, acc) for a in range(NSEL)]
        items = works(at, [(y, (x, y)) for y in range(1, CY - 1)], BLOCK, vel, dz, mv)
        items.insert(len(items) // 3, lambda: transpose(plane(x), mt))
        if not last:
            items.insert(2 * len(items) // 3, lambda: survey(plane(x + 1), picker, shift, vel_n, dz_n))
        interleave(items, todo)

    survey(plane(1), picker, shift, vel_a, dz_a)
    stage(1, 0, dots=False)
    stage(2, 1, first=True)

    def pair(j, carry):
        stage(2 * j + 3, 0)
        stage(2 * j + 4, 1)
        return carry

    lax.fori_loop(0, 2, pair, 0)
    for a in range(NSEL):
        product(a, BLOCK, mt_b, mv_b, acc, acc)


def boundary_kernel(conv, core, modes, near, far, yface, start, theirs, mine,
                    xface, acc, picker, shift, vel_a, vel_b, dz_a, dz_b, mt_a, mt_b, mv_a, mv_b):
    me = core[0]
    constants(conv, picker, shift)
    xface[:, pl.ds(1 - me, 1)] = near[...]
    xface[:, pl.ds(me, 1)] = far[...]
    sets = [(vel_a, dz_a, mt_a, mv_a), (vel_b, dz_b, mt_b, mv_b)]

    def at(c, x, y, lanes):
        if x in (-1, CX):
            return xface[c, 1 if x == CX else 0, y, :, lanes]
        if y in (-1, CY):
            return yface[c, x, 1 if y == CY else 0, :, lanes]
        return modes[c, x, y, :, lanes]

    edge = [(x, y) for y in (0, CY - 1) for x in range(1, CX - 1)]
    work = [edge] + [[(x, y) for y in range(CY)] for x in (0, CX - 1)]

    def rows(k):
        if k == 0:
            half = len(edge) * NZ // 2
            return [
                jnp.concatenate([modes[c, 1 : CX - 1, y].reshape(half, M) for y in (0, CY - 1)], axis=0)
                for c in range(3)
            ]
        return [modes[c, work[k][0][0]].reshape(BLOCK, M) for c in range(3)]

    survey(rows(0), picker, shift, vel_a, dz_a)
    for k in range(3):
        vel, dz, mt, mv = sets[k % 2]
        vel_n, dz_n, mt_r, mv_r = sets[(k + 1) % 2]
        n = len(work[k]) * NZ
        todo = []
        if k > 0:
            before = len(work[k - 1]) * NZ
            source = start if k == 1 else acc
            todo = [lambda a=a: product(a, before, mt_r, mv_r, source, acc) for a in range(NSEL)]
        items = works(at, list(enumerate(work[k])), n, vel, dz, mv)
        items.insert(len(items) // 3, lambda: transpose(rows(k), mt))
        if k < 2:
            items.insert(2 * len(items) // 3, lambda: survey(rows(k + 1), picker, shift, vel_n, dz_n))
        interleave(items, todo)
    for a in range(NSEL):
        product(a, BLOCK, mt_a, mv_a, acc, acc)

    def finish(a, carry):
        block = acc[a]
        block = (block - block.T).reshape(M // 8, 2, 4, M)
        theirs[a] = jnp.where(me == 0, block[:, 1], block[:, 0]).astype(jnp.bfloat16)
        mine[a] = jnp.where(me == 0, block[:, 0], block[:, 1])
        return carry

    lax.fori_loop(0, NSEL, finish, 0)


def faces_kernel(core, modes, near, far, yface, sems):
    last = (CX - 1) * core[0]
    copies = [
        pltpu.make_async_copy(modes.at[:, pl.ds(last, 1)], far, sems.at[0]),
        pltpu.make_async_copy(modes.at[:, pl.ds(CX - 1 - last, 1)], near, sems.at[1]),
        pltpu.make_async_copy(modes.at[:, :, CY - 1 : CY], yface.at[:, :, 0:1], sems.at[2]),
        pltpu.make_async_copy(modes.at[:, :, 0:1], yface.at[:, :, 1:2], sems.at[3]),
    ]
    for copy in copies:
        copy.start()
    for copy in copies:
        copy.wait()


SMEM = pl.BlockSpec(memory_space=pltpu.SMEM)
HBM = pl.BlockSpec(memory_space=pltpu.HBM)
VMEM = pl.BlockSpec(memory_space=pltpu.VMEM)
WORK = (
    [pltpu.VMEM((M, 128), jnp.bfloat16), pltpu.VMEM((BLOCK, BLOCK), jnp.bfloat16)]
    + [pltpu.VMEM((3, BLOCK, 128), jnp.float32)] * 2
    + [pltpu.VMEM((3, BLOCK, M), jnp.float32)] * 2
)
BUFFERS = [pltpu.VMEM((M, 3 * BLOCK), jnp.bfloat16)] * 2 + [pltpu.VMEM((NSEL, 3 * BLOCK, M), jnp.bfloat16)] * 2


def faces(core, modes):
    return pl.pallas_call(
        faces_kernel,
        out_shape=(
            pltpu.VMEM((3, 1, CY, NZ, M), jnp.bfloat16),
            pltpu.VMEM((3, 1, CY, NZ, M), jnp.bfloat16),
            pltpu.VMEM((3, CX, 2, NZ, M), jnp.bfloat16),
        ),
        in_specs=[SMEM, HBM],
        out_specs=(VMEM, VMEM, VMEM),
        scratch_shapes=[pltpu.SemaphoreType.DMA((4,))],
        compiler_params=pltpu.CompilerParams(vmem_limit_bytes=VMEM_LIMIT),
        name="faces",
    )(core, modes)


def interior(convecting, modes):
    return pl.pallas_call(
        interior_kernel,
        out_shape=pltpu.VMEM((NSEL, M, M), jnp.float32),
        in_specs=[SMEM, VMEM],
        out_specs=VMEM,
        scratch_shapes=WORK + BUFFERS,
        compiler_params=pltpu.CompilerParams(vmem_limit_bytes=VMEM_LIMIT),
        name="interior",
    )(convecting, modes)


def boundary(convecting, core, modes, near, far, yface, start):
    return pl.pallas_call(
        boundary_kernel,
        out_shape=(
            pltpu.VMEM((NSEL, M // 8, 4, M), jnp.bfloat16),
            pltpu.VMEM((NSEL, M // 8, 4, M), jnp.float32),
        ),
        in_specs=[SMEM, SMEM] + [VMEM] * 5,
        out_specs=(VMEM, VMEM),
        scratch_shapes=[pltpu.VMEM((3, 2, CY, NZ, M), jnp.bfloat16), pltpu.VMEM((NSEL, M, M), jnp.float32)]
        + WORK + BUFFERS,
        compiler_params=pltpu.CompilerParams(vmem_limit_bytes=VMEM_LIMIT),
        name="boundary",
    )(convecting, core, modes, near, far, yface, start)


def shards(modes, convecting):
    swap = [(0, 1), (1, 0)]
    across = [(s, (s + 1) % 64 if s % 2 else (s - 1) % 64) for s in range(64)]
    core = lax.axis_index("core").reshape(1).astype(jnp.int32)
    near, far, yface = faces(core, modes)
    far = lax.ppermute(far, SP, across)
    near = lax.ppermute(near, "core", swap)
    yface = lax.ppermute(yface, "yl", swap)
    start = interior(convecting, modes)
    theirs, mine = boundary(convecting, core, modes, near, far, yface, start)
    paired = (mine + lax.ppermute(theirs, "core", swap).astype(jnp.float32)).astype(jnp.bfloat16)
    spread = lax.all_to_all(paired, SP[:3], split_axis=1, concat_axis=0, tiled=True)
    owned = spread.reshape(32, NSEL, 4, M).astype(jnp.float32).sum(0)
    owned = owned + lax.ppermute(owned, "yl", swap)
    return owned * (0.25 / 512.0)


def solution(mesh):
    fine = Mesh(mesh.devices.reshape(2, 4, 2, 4, 2), ("yl",) + SP)
    placed = (P(None, SP, "yl", None, None), P())
    return jax.shard_map(
        shards, mesh=fine, in_specs=placed, out_specs=P(None, SP, None), check_vma=False
    )
```
